32 devices in a mesh: prompts: 4 (over y, core), units: 8 (over z, x).
Axes of the slice: x: 2, y: 2, z: 4, core: 2. Of those that a mesh axis runs over, the one named last changes fastest.
Arguments:
- hidden_acts: bfloat16 [16, 2048, 14336], P('prompts', None, 'units'), may hold values from -6 to 6
- out_grads: bfloat16 [16, 2048, 4096], P('prompts', None, 'units'), may hold values from -6 to 6
- proj_in: bfloat16 [14336, 64], P('units'), may hold values from -0.29231698 to 0.29231698
- proj_out: bfloat16 [4096, 64], P('units'), may hold values from -0.09375 to 0.09375
- lengths: int32 [16], P('prompts'), may hold values from 256 to 2048
- val_grads: float32 [256, 4096], P('prompts', 'units'), may hold values from -6 to 6
Outputs:
- scores: float32 [16, 256], P('prompts')
The draws below stay inside these ranges and needn't reach their ends.
All inputs are finite; a program needn't handle non-finite values.
Results may differ from the reference program's by a relative error of at most 0.0003.
Values sent between devices are 32-bit elements; how exact they have to be, the bound alone decides.
A program may use at most 128 MiB of HBM per device.

```python
import jax
import jax.numpy as jnp
from jax import lax

D = 4096
FF = 14336
RANK = 64
LEN = 2048
TRAIN = 16
VAL = 256
FEAT = 4096


def draw_proj_in(key, part):
    first, second = jax.random.split(key)
    base = jnp.clip(jax.random.normal(first, (FF, RANK), jnp.float32), -6.0, 6.0)
    jitter = jax.random.uniform(second, (RANK,), jnp.float32, -0.5, 0.5)
    column = 10.0 ** ((jnp.arange(RANK, dtype=jnp.float32) + jitter) / RANK)
    return (base * column[None, :] / jnp.sqrt(jnp.float32(FF) * 3.0)).astype(jnp.bfloat16)


def place_ends(array, rng, smallest, top_value):
    extent = array.shape
    index_at = [jax.random.randint(jax.random.fold_in(rng, axis), (), 0, extent[axis]) for axis in range(len(extent))]
    array = array.at[tuple(index_at)].set(smallest)
    longest = extent.index(max(extent))
    index_at[longest] = (index_at[longest] + 1) % extent[longest]
    return array.at[tuple(index_at)].set(top_value)


def shard_levels(rng, shape, shards, smallest, largest):
    def one(position, parts):
        draws = jax.random.uniform(jax.random.fold_in(jax.random.fold_in(rng, 6), position), (parts,), jnp.float32, smallest / len(shards), largest / len(shards))
        return jnp.repeat(jnp.exp(draws), shape[position] // parts).reshape((-1,) + (1,) * (len(shape) - position - 1))

    level = one(*shards[0])
    for cut in shards[1:]:
        level = level * one(*cut)
    return level


def noise(rng, shape, deviation, bound, shards=(), kind=jnp.bfloat16):
    factor_of = shard_levels(rng, shape, shards, -0.22, 0.18) if shards else 1.0
    drawn = jax.random.normal(rng, shape, jnp.float32) * deviation * factor_of
    return jnp.minimum(jnp.maximum(drawn, -bound), bound).astype(kind)


def setup_inputs(seed: int = 0) -> dict:
    seeds = jax.random.split(jax.random.key(seed), 7)
    hidden_acts = noise(seeds[0], (TRAIN, LEN, FF), 1.0, 6.0, ((0, 4), (2, 8)))
    out_grads = noise(seeds[1], (TRAIN, LEN, D), 1.0, 6.0, ((0, 4), (2, 8)))
    proj_in = draw_proj_in(jax.random.fold_in(seeds[6], 71), 0)
    proj_out = noise(seeds[3], (D, RANK), D ** -0.5, 0.09375, ((0, 8),))
    lengths = place_ends(jax.random.randint(seeds[4], (TRAIN,), LEN // 8, LEN + 1), jax.random.fold_in(seeds[4], 1), LEN // 8, LEN).astype(jnp.int32)
    val_grads = noise(seeds[5], (VAL, FEAT), 1.0, 6.0, ((0, 4), (1, 8)), jnp.float32)
    return {"hidden_acts": hidden_acts, "out_grads": out_grads, "proj_in": proj_in, "proj_out": proj_out, "lengths": lengths, "val_grads": val_grads}


def one_prompt(item, proj_in, proj_out):
    acts, grads_out, length = item
    inner = jnp.dot(acts, proj_in, preferred_element_type=jnp.float32)
    outer = jnp.dot(grads_out, proj_out, preferred_element_type=jnp.float32)
    valid = (jnp.arange(acts.shape[0], dtype=jnp.int32) < length).astype(jnp.float32)
    inner = inner * valid[:, None]
    full = jnp.dot(inner.T, outer, precision=lax.Precision.HIGHEST, preferred_element_type=jnp.float32)
    return full.reshape(-1)

def reference(hidden_acts, out_grads, proj_in, proj_out, lengths, val_grads):
    grads = lax.map(lambda item: one_prompt(item, proj_in, proj_out), (hidden_acts, out_grads, lengths))
    dots = jnp.dot(grads, val_grads.T, precision=lax.Precision.HIGHEST, preferred_element_type=jnp.float32)
    squares = lax.optimization_barrier(jnp.sum(grads * grads, axis=1))
    return dots / jnp.sqrt(squares + 1e-06)[:, None]
```

```python
import functools
import math

import jax
import jax.numpy as jnp
from jax import lax
from jax.experimental import pallas as pl
from jax.experimental.pallas import tpu as pltpu
from jax.sharding import PartitionSpec as P

MESH = pl.DeviceIdType.MESH
HIGHEST = lax.Precision.HIGHEST
LANES = 128
SUB = 128


def kernel(
    cfg,
    acts, grads, win, wout, lens, val,
    out,
    abuf, gbuf, wi, wo, sx, own, rx, pre, suf, psend, ssend, macc, gsend, grecv, vall, dsend, drecv,
    hbm_sem, x_s, x_r, pre_s, pre_r, suf_s, suf_r, v_s, v_r, v_l, g_s, g_r, d_s, d_r,
):
    N, I, O, Q = cfg["N"], cfg["I"], cfg["O"], cfg["Q"]
    ct, ncb, nb, spc = cfg["ct"], cfg["ncb"], cfg["nb"], cfg["spc"]
    seq, p_here, p_own, rank = cfg["seq"], cfg["p_here"], cfg["p_own"], cfg["rank"]
    rows_own = ncb * ct
    half = ct // 2
    K = I * ncb
    me = lax.axis_index("units")
    q = lax.axis_index("prompts")
    o = me // I
    i = me % I

    barrier = pltpu.get_barrier_semaphore()
    for d in range(1, N):
        pl.semaphore_signal(barrier, inc=1, device_id={"units": (me + d) % N}, device_id_type=MESH)
    for d in range(1, Q):
        pl.semaphore_signal(barrier, inc=1, device_id={"prompts": (q + d) % Q}, device_id_type=MESH)

    def fetch(k):
        owner = (i + 1 + k // ncb) % I
        row0 = pl.multiple_of(owner * rows_own + (k % ncb) * ct, ct)
        slot = k % 2
        return (
            pltpu.make_async_copy(acts.at[pl.ds(row0, ct)], abuf.at[slot], hbm_sem.at[slot, 0]),
            pltpu.make_async_copy(grads.at[pl.ds(row0, ct)], gbuf.at[slot], hbm_sem.at[slot, 1]),
        )

    for copy in fetch(0):
        copy.start()

    zero_i = jnp.zeros(win.shape, win.dtype)
    wi[0] = jnp.concatenate([win[...], zero_i], axis=1)
    wi[1] = jnp.concatenate([zero_i, win[...]], axis=1)
    zero_o = jnp.zeros(wout.shape, wout.dtype)
    wo[0] = jnp.concatenate([wout[...], zero_o], axis=1)
    wo[1] = jnp.concatenate([zero_o, wout[...]], axis=1)
    macc[...] = jnp.zeros_like(macc)

    vrows = val.shape[0]
    mine = vall.at[pl.ds(pl.multiple_of(q * vrows, vrows), vrows)]
    val_own = pltpu.make_async_copy(val, mine, v_l)
    val_own.start()

    pl.semaphore_wait(barrier, N - 1 + Q - 1)

    def val_copy(d):
        return pltpu.make_async_remote_copy(
            src_ref=val, dst_ref=mine, send_sem=v_s.at[d - 1], recv_sem=v_r.at[d - 1],
            device_id={"prompts": (q + d) % Q}, device_id_type=MESH,
        )

    for d in range(1, Q):
        val_copy(d).start()

    def project(k, store):
        @pl.when(k + 1 < K)
        def _():
            for copy in fetch(k + 1):
                copy.start()

        for copy in fetch(k):
            copy.wait()
        slot = k % 2
        for side, (buf, w) in enumerate(((abuf, wi), (gbuf, wo))):
            part = jnp.dot(buf[slot, :half], w[0], preferred_element_type=jnp.float32)
            part += jnp.dot(buf[slot, half:], w[1], preferred_element_type=jnp.float32)
            for s in range(spc):
                store(s, side, part[s * SUB : (s + 1) * SUB])

    def x_copy(e, b):
        return pltpu.make_async_remote_copy(
            src_ref=sx.at[e, b], dst_ref=rx.at[e, b], send_sem=x_s.at[e, b], recv_sem=x_r.at[e, b],
            device_id={"units": o * I + (i + 1 + e) % I}, device_id_type=MESH,
        )

    def first(k, carry):
        e = k // ncb
        base = (k % ncb) * spc

        def store(s, side, x):
            sx[e, base + s, side] = x

        project(k, store)
        for s in range(spc):
            x_copy(e, base + s).start()
        return carry

    lax.fori_loop(0, (I - 1) * ncb, first, 0)

    def second(c, carry):
        def store(s, side, x):
            own[c * spc + s, side] = x

        project((I - 1) * ncb + c, store)
        return carry

    lax.fori_loop(0, ncb, second, 0)

    def right_copy(b):
        return pltpu.make_async_remote_copy(
            src_ref=psend.at[b], dst_ref=pre.at[b], send_sem=pre_s.at[b], recv_sem=pre_r.at[b],
            device_id={"units": (me + I) % N}, device_id_type=MESH,
        )

    def left_copy(b):
        return pltpu.make_async_remote_copy(
            src_ref=ssend.at[b], dst_ref=suf.at[b], send_sem=suf_s.at[b], recv_sem=suf_r.at[b],
            device_id={"units": (me + N - I) % N}, device_id_type=MESH,
        )

    def third(t, carry):
        @pl.when(t < nb)
        def _():
            for e in range(I - 1):
                x_copy(e, t).wait_recv()
            a = own[t, 0]
            g = own[t, 1]
            for e in range(I - 1):
                a += rx[e, t, 0]
                g += rx[e, t, 1]
            own[t, 0] = a
            tok0 = (t // spc) * ct
            pos = tok0 % seq + (t % spc) * SUB + lax.broadcasted_iota(jnp.int32, (SUB, LANES), 0)
            lane = lax.broadcasted_iota(jnp.int32, (SUB, LANES), 1)
            pos = pos + jnp.where(lane < rank, 0, half)
            length = lens[i * p_own + tok0 // seq]
            own[t, 1] = jnp.where(pos < length, g, 0.0)

        br = t - o

        @pl.when((br >= 0) & (br < nb))
        def _():
            @pl.when(o == 0)
            def _():
                psend[br] = own[br, 0]

            @pl.when(o > 0)
            def _():
                right_copy(br).wait_recv()
                psend[br] = own[br, 0] + pre[br]

            @pl.when(o < O - 1)
            def _():
                right_copy(br).start()

        bl = t - (O - 1 - o)

        @pl.when((bl >= 0) & (bl < nb))
        def _():
            @pl.when(o == O - 1)
            def _():
                ssend[bl] = own[bl, 0]

            @pl.when(o < O - 1)
            def _():
                left_copy(bl).wait_recv()
                ssend[bl] = own[bl, 0] + suf[bl]

            @pl.when(o > 0)
            def _():
                left_copy(bl).start()

        b = t - (O - 1)

        @pl.when(b >= 0)
        def _():
            def add(x):
                p = ((b // spc) * ct) // seq
                macc[p] += lax.dot_general(
                    x, own[b, 1], (((0,), (0,)), ((), ())), precision=HIGHEST,
                    preferred_element_type=jnp.float32,
                )

            @pl.when(o < O - 1)
            def _():
                add(psend[b] + suf[b])

            @pl.when(o == O - 1)
            def _():
                add(psend[b])

        return carry

    lax.fori_loop(0, nb + O - 1, third, 0)

    grows = gsend.shape[2]
    for p in range(p_own):
        m = macc[p]
        g = m[:rank, :rank] + m[rank:, rank:]
        g2 = jnp.concatenate([g, g], axis=1)
        for n in range(N):
            gsend[n, p] = g2[n * grows : (n + 1) * grows]

    def g_copy(d):
        to = (me + d) % N
        return pltpu.make_async_remote_copy(
            src_ref=gsend.at[to], dst_ref=grecv.at[me], send_sem=g_s.at[d - 1], recv_sem=g_r.at[d - 1],
            device_id={"units": to}, device_id_type=MESH,
        )

    for d in range(1, N):
        g_copy(d).start()
    grecv[me] = gsend[me]
    val_own.wait()
    for d in range(1, Q):
        val_copy(d).wait()
    for d in range(1, N):
        g_copy(d).wait()

    lane = lax.broadcasted_iota(jnp.int32, (1, LANES), 1)
    rows = []
    for p in range(p_here):
        x, k = p // p_own, p % p_own
        s = grecv[x, k]
        for z in range(1, O):
            s += grecv[z * I + x, k]
        flat = [
            jnp.where(lane < rank, s[2 * r : 2 * r + 1], s[2 * r + 1 : 2 * r + 2])
            for r in range(grows // 2)
        ]
        rows.append(jnp.concatenate(flat, axis=1))
    pad = dsend.shape[0] - p_here
    feat = jnp.concatenate(rows + [jnp.zeros((pad, rows[0].shape[1]), jnp.float32)], axis=0)
    nval = vall.shape[0]
    dsend[:, :nval] = lax.dot_general(
        feat, vall[...], (((1,), (1,)), ((), ())), precision=HIGHEST,
        preferred_element_type=jnp.float32,
    )
    dsend[:, nval:] = jnp.broadcast_to(
        jnp.sum(feat * feat, axis=1, keepdims=True), (dsend.shape[0], LANES)
    )

    def d_copy(d):
        return pltpu.make_async_remote_copy(
            src_ref=dsend, dst_ref=drecv.at[me], send_sem=d_s.at[d - 1], recv_sem=d_r.at[d - 1],
            device_id={"units": (me + d) % N}, device_id_type=MESH,
        )

    for d in range(1, N):
        d_copy(d).start()
    drecv[me] = dsend[...]

    def drain(b, carry):
        for e in range(I - 1):
            x_copy(e, b).wait_send()

        @pl.when(o < O - 1)
        def _():
            right_copy(b).wait_send()

        @pl.when(o > 0)
        def _():
            left_copy(b).wait_send()

        return carry

    lax.fori_loop(0, nb, drain, 0)
    for d in range(1, N):
        d_copy(d).wait()
    total = drecv[0]
    for n in range(1, N):
        total += drecv[n]
    out[...] = total[:p_here, :nval] / jnp.sqrt(total[:p_here, nval : nval + 1] + 1e-06)


def per_device(inner, hidden_acts, out_grads, proj_in, proj_out, lengths, val_grads):
    p_here, seq, units_here = hidden_acts.shape
    rank = proj_in.shape[1]
    N, Q = lax.axis_size("units"), lax.axis_size("prompts")
    I = inner
    O = N // I
    p_own = p_here // I
    rows_own = p_own * seq
    ct = min(1024, seq)
    ncb = rows_own // ct
    spc = ct // 2 // SUB
    nb = ncb * spc
    feats = val_grads.shape[1]
    grows = feats // rank
    nval = val_grads.shape[0] * Q
    cfg = dict(
        N=N, I=I, O=O, Q=Q, ct=ct, ncb=ncb, nb=nb, spc=spc, seq=seq, p_here=p_here, p_own=p_own, rank=rank
    )
    f32 = jnp.float32
    dma = pltpu.SemaphoreType.DMA
    block = (SUB, LANES)
    drows = -(-p_here // 8) * 8
    vmem = pl.BlockSpec(memory_space=pltpu.VMEM)
    hbm = pl.BlockSpec(memory_space=pl.ANY)
    return pl.pallas_call(
        functools.partial(kernel, cfg),
        out_shape=jax.ShapeDtypeStruct((p_here, nval), f32),
        in_specs=[hbm, hbm, vmem, vmem, pl.BlockSpec(memory_space=pltpu.SMEM), vmem],
        out_specs=vmem,
        scratch_shapes=[
            pltpu.VMEM((2, ct, units_here), hidden_acts.dtype),
            pltpu.VMEM((2, ct, out_grads.shape[2]), out_grads.dtype),
            pltpu.VMEM((2, units_here, LANES), proj_in.dtype),
            pltpu.VMEM((2, out_grads.shape[2], LANES), proj_out.dtype),
            pltpu.VMEM((I - 1, nb, 2) + block, f32),
            pltpu.VMEM((nb, 2) + block, f32),
            pltpu.VMEM((I - 1, nb, 2) + block, f32),
            pltpu.VMEM((nb,) + block, f32),
            pltpu.VMEM((nb,) + block, f32),
            pltpu.VMEM((nb,) + block, f32),
            pltpu.VMEM((nb,) + block, f32),
            pltpu.VMEM((p_own, LANES, LANES), f32),
            pltpu.VMEM((N, p_own, grows, LANES), f32),
            pltpu.VMEM((N, p_own, grows, LANES), f32),
            pltpu.VMEM((nval, feats), f32),
            pltpu.VMEM((drows, nval + LANES), f32),
            pltpu.VMEM((N, drows, nval + LANES), f32),
            dma((2, 2)),
            dma((I - 1, nb)), dma((I - 1, nb)),
            dma((nb,)), dma((nb,)), dma((nb,)), dma((nb,)),
            dma((Q - 1,)), dma((Q - 1,)), dma,
            dma((N - 1,)), dma((N - 1,)), dma((N - 1,)), dma((N - 1,)),
        ],
        compiler_params=pltpu.CompilerParams(
            collective_id=0, has_side_effects=True, vmem_limit_bytes=60 * 1024 * 1024
        ),
    )(
        hidden_acts.reshape(p_here * seq, units_here),
        out_grads.reshape(p_here * seq, out_grads.shape[2]),
        proj_in, proj_out, lengths, val_grads,
    )


def solution(mesh):
    inner = 2 ** (int(math.log2(mesh.shape["units"])) // 2)
    in_specs = (
        P("prompts", None, "units"),
        P("prompts", None, "units"),
        P("units", None),
        P("units", None),
        P("prompts"),
        P("prompts", "units"),
    )
    return jax.shard_map(
        functools.partial(per_device, inner), mesh=mesh, in_specs=in_specs,
        out_specs=P("prompts", None), check_vma=False,
    )
```

```python
import functools
import math

import jax
import jax.numpy as jnp
from jax import lax
from jax.experimental import pallas as pl
from jax.experimental.pallas import tpu as pltpu
from jax.sharding import PartitionSpec as P

MESH = pl.DeviceIdType.MESH
HIGHEST = lax.Precision.HIGHEST
LANES = 128
SKEW = 2
SUB = 128


def kernel(
    cfg,
    acts, grads, win, wout, lens, val,
    out,
    abuf, gbuf, wi, wo, sx, own, rx, pre, suf, psend, ssend, macc, gsend, grecv, vall, dsend, drecv,
    hbm_sem, x_s, x_r, pre_s, pre_r, suf_s, suf_r, v_s, v_r, v_l, g_s, g_r, d_s, d_r,
):
    N, I, O, Q = cfg["N"], cfg["I"], cfg["O"], cfg["Q"]
    ct, ncb, nb, spc = cfg["ct"], cfg["ncb"], cfg["nb"], cfg["spc"]
    seq, p_here, p_own, rank = cfg["seq"], cfg["p_here"], cfg["p_own"], cfg["rank"]
    rows_own = ncb * ct
    half = ct // 2
    K = I * ncb
    me = lax.axis_index("units")
    q = lax.axis_index("prompts")
    o = me // I
    i = me % I

    barrier = pltpu.get_barrier_semaphore()
    for d in range(1, N):
        pl.semaphore_signal(barrier, inc=1, device_id={"units": (me + d) % N}, device_id_type=MESH)
    for d in range(1, Q):
        pl.semaphore_signal(barrier, inc=1, device_id={"prompts": (q + d) % Q}, device_id_type=MESH)

    def fetch(k):
        owner = (i + 1 + k // ncb) % I
        row0 = pl.multiple_of(owner * rows_own + (k % ncb) * ct, ct)
        slot = k % 2
        return (
            pltpu.make_async_copy(acts.at[pl.ds(row0, ct)], abuf.at[slot], hbm_sem.at[slot, 0]),
            pltpu.make_async_copy(grads.at[pl.ds(row0, ct)], gbuf.at[slot], hbm_sem.at[slot, 1]),
        )

    for copy in fetch(0):
        copy.start()

    for w, dst in ((win, wi), (wout, wo)):
        t = w[...].astype(jnp.float32)
        zero = jnp.zeros_like(t)
        dst[0] = jnp.concatenate([t, zero], axis=0).T.astype(dst.dtype)
        dst[1] = jnp.concatenate([zero, t], axis=0).T.astype(dst.dtype)
    macc[...] = jnp.zeros_like(macc)

    vrows = val.shape[0]
    mine = vall.at[pl.ds(pl.multiple_of(q * vrows, vrows), vrows)]
    val_own = pltpu.make_async_copy(val, mine, v_l)
    val_own.start()

    def val_copy(d):
        return pltpu.make_async_remote_copy(
            src_ref=val, dst_ref=mine, send_sem=v_s.at[d - 1], recv_sem=v_r.at[d - 1],
            device_id={"prompts": (q + d) % Q}, device_id_type=MESH,
        )

    def project(k, store):
        @pl.when(k + 1 < K)
        def _():
            for copy in fetch(k + 1):
                copy.start()

        for copy in fetch(k):
            copy.wait()
        slot = k % 2
        for side, (buf, w) in enumerate(((abuf, wi), (gbuf, wo))):
            part = jnp.dot(buf[slot, :half], w[0], preferred_element_type=jnp.float32)
            part += jnp.dot(buf[slot, half:], w[1], preferred_element_type=jnp.float32)
            for s in range(spc):
                store(s, side, part[s * SUB : (s + 1) * SUB])

    def x_copy(e, b):
        return pltpu.make_async_remote_copy(
            src_ref=sx.at[e, b], dst_ref=rx.at[e, b], send_sem=x_s.at[e, b], recv_sem=x_r.at[e, b],
            device_id={"units": o * I + (i + 1 + e) % I}, device_id_type=MESH,
        )

    def first_compute(k):
        def store(s, side, x):
            sx[k // ncb, (k % ncb) * spc + s, side] = x

        project(k, store)

    def first_send(k):
        for s in range(spc):
            x_copy(k // ncb, (k % ncb) * spc + s).start()

    def first(k, carry):
        first_compute(k)
        first_send(k)
        return carry

    first_compute(0)
    pl.semaphore_wait(barrier, N - 1 + Q - 1)
    first_send(0)
    for d in range(1, Q):
        val_copy(d).start()
    lax.fori_loop(1, (I - 1) * ncb, first, 0)

    def second(c, carry):
        def store(s, side, x):
            own[c * spc + s, side] = x

        project((I - 1) * ncb + c, store)
        return carry

    lax.fori_loop(0, ncb, second, 0)

    def right_copy(b):
        return pltpu.make_async_remote_copy(
            src_ref=psend.at[b], dst_ref=pre.at[b], send_sem=pre_s.at[b], recv_sem=pre_r.at[b],
            device_id={"units": (me + I) % N}, device_id_type=MESH,
        )

    def left_copy(b):
        return pltpu.make_async_remote_copy(
            src_ref=ssend.at[b], dst_ref=suf.at[b], send_sem=suf_s.at[b], recv_sem=suf_r.at[b],
            device_id={"units": (me + N - I) % N}, device_id_type=MESH,
        )

    def third(t, carry):
        @pl.when(t < nb)
        def _():
            for e in range(I - 1):
                x_copy(e, t).wait_recv()
            a = own[t, 0]
            g = own[t, 1]
            for e in range(I - 1):
                a += rx[e, t, 0]
                g += rx[e, t, 1]
            own[t, 0] = a
            tok0 = (t // spc) * ct
            pos = tok0 % seq + (t % spc) * SUB + lax.broadcasted_iota(jnp.int32, (SUB, LANES), 0)
            lane = lax.broadcasted_iota(jnp.int32, (SUB, LANES), 1)
            pos = pos + jnp.where(lane < rank, 0, half)
            length = lens[i * p_own + tok0 // seq]
            own[t, 1] = jnp.where(pos < length, g, 0.0)

        br = t - SKEW * o

        @pl.when((br >= 0) & (br < nb))
        def _():
            @pl.when(o == 0)
            def _():
                psend[br] = own[br, 0]

            @pl.when(o > 0)
            def _():
                right_copy(br).wait_recv()
                psend[br] = own[br, 0] + pre[br]

            @pl.when(o < O - 1)
            def _():
                right_copy(br).start()

        bl = t - SKEW * (O - 1 - o)

        @pl.when((bl >= 0) & (bl < nb))
        def _():
            @pl.when(o == O - 1)
            def _():
                ssend[bl] = own[bl, 0]

            @pl.when(o < O - 1)
            def _():
                left_copy(bl).wait_recv()
                ssend[bl] = own[bl, 0] + suf[bl]

            @pl.when(o > 0)
            def _():
                left_copy(bl).start()

        b = t - SKEW * (O - 1)

        @pl.when(b >= 0)
        def _():
            def add(x):
                p = ((b // spc) * ct) // seq
                macc[p] += lax.dot_general(
                    x, own[b, 1], (((0,), (0,)), ((), ())), precision=HIGHEST,
                    preferred_element_type=jnp.float32,
                )

            @pl.when(o < O - 1)
            def _():
                add(psend[b] + suf[b])

            @pl.when(o == O - 1)
            def _():
                add(psend[b])

        return carry

    lax.fori_loop(0, nb + SKEW * (O - 1), third, 0)

    grows = gsend.shape[2]
    for p in range(p_own):
        m = macc[p]
        g = m[:rank, :rank] + m[rank:, rank:]
        g2 = jnp.concatenate([g, g], axis=1)
        for n in range(N):
            gsend[n, p] = g2[n * grows : (n + 1) * grows]

    def g_copy(d):
        to = (me + d) % N
        return pltpu.make_async_remote_copy(
            src_ref=gsend.at[to], dst_ref=grecv.at[me], send_sem=g_s.at[d - 1], recv_sem=g_r.at[d - 1],
            device_id={"units": to}, device_id_type=MESH,
        )

    for d in range(1, N):
        g_copy(d).start()
    grecv[me] = gsend[me]
    val_own.wait()
    for d in range(1, Q):
        val_copy(d).wait()
    for d in range(1, N):
        g_copy(d).wait()

    lane = lax.broadcasted_iota(jnp.int32, (1, LANES), 1)
    rows = []
    for p in range(p_here):
        x, k = p // p_own, p % p_own
        s = grecv[x, k]
        for z in range(1, O):
            s += grecv[z * I + x, k]
        flat = [
            jnp.where(lane < rank, s[2 * r : 2 * r + 1], s[2 * r + 1 : 2 * r + 2])
            for r in range(grows // 2)
        ]
        rows.append(jnp.concatenate(flat, axis=1))
    pad = dsend.shape[0] - p_here
    feat = jnp.concatenate(rows + [jnp.zeros((pad, rows[0].shape[1]), jnp.float32)], axis=0)
    nval = vall.shape[0]
    dsend[:, :nval] = lax.dot_general(
        feat, vall[...], (((1,), (1,)), ((), ())), precision=HIGHEST,
        preferred_element_type=jnp.float32,
    )
    dsend[:, nval:] = jnp.broadcast_to(
        jnp.sum(feat * feat, axis=1, keepdims=True), (dsend.shape[0], LANES)
    )

    def d_copy(d):
        return pltpu.make_async_remote_copy(
            src_ref=dsend, dst_ref=drecv.at[me], send_sem=d_s.at[d - 1], recv_sem=d_r.at[d - 1],
            device_id={"units": (me + d) % N}, device_id_type=MESH,
        )

    for d in range(1, N):
        d_copy(d).start()
    drecv[me] = dsend[...]

    def drain(b, carry):
        for e in range(I - 1):
            x_copy(e, b).wait_send()

        @pl.when(o < O - 1)
        def _():
            right_copy(b).wait_send()

        @pl.when(o > 0)
        def _():
            left_copy(b).wait_send()

        return carry

    lax.fori_loop(0, nb, drain, 0)
    for d in range(1, N):
        d_copy(d).wait()
    total = drecv[0]
    for n in range(1, N):
        total += drecv[n]
    out[...] = total[:p_here, :nval] / jnp.sqrt(total[:p_here, nval : nval + 1] + 1e-06)


def per_device(inner, hidden_acts, out_grads, proj_in, proj_out, lengths, val_grads):
    p_here, seq, units_here = hidden_acts.shape
    rank = proj_in.shape[1]
    N, Q = lax.axis_size("units"), lax.axis_size("prompts")
    I = inner
    O = N // I
    p_own = p_here // I
    rows_own = p_own * seq
    ct = min(1024, seq)
    ncb = rows_own // ct
    spc = ct // 2 // SUB
    nb = ncb * spc
    feats = val_grads.shape[1]
    grows = feats // rank
    nval = val_grads.shape[0] * Q
    cfg = dict(
        N=N, I=I, O=O, Q=Q, ct=ct, ncb=ncb, nb=nb, spc=spc, seq=seq, p_here=p_here, p_own=p_own, rank=rank
    )
    f32 = jnp.float32
    dma = pltpu.SemaphoreType.DMA
    block = (SUB, LANES)
    drows = -(-p_here // 8) * 8
    vmem = pl.BlockSpec(memory_space=pltpu.VMEM)
    hbm = pl.BlockSpec(memory_space=pl.ANY)
    return pl.pallas_call(
        functools.partial(kernel, cfg),
        out_shape=jax.ShapeDtypeStruct((p_here, nval), f32),
        in_specs=[hbm, hbm, vmem, vmem, pl.BlockSpec(memory_space=pltpu.SMEM), vmem],
        out_specs=vmem,
        scratch_shapes=[
            pltpu.VMEM((2, ct, units_here), hidden_acts.dtype),
            pltpu.VMEM((2, ct, out_grads.shape[2]), out_grads.dtype),
            pltpu.VMEM((2, units_here, LANES), proj_in.dtype),
            pltpu.VMEM((2, out_grads.shape[2], LANES), proj_out.dtype),
            pltpu.VMEM((I - 1, nb, 2) + block, f32),
            pltpu.VMEM((nb, 2) + block, f32),
            pltpu.VMEM((I - 1, nb, 2) + block, f32),
            pltpu.VMEM((nb,) + block, f32),
            pltpu.VMEM((nb,) + block, f32),
            pltpu.VMEM((nb,) + block, f32),
            pltpu.VMEM((nb,) + block, f32),
            pltpu.VMEM((p_own, LANES, LANES), f32),
            pltpu.VMEM((N, p_own, grows, LANES), f32),
            pltpu.VMEM((N, p_own, grows, LANES), f32),
            pltpu.VMEM((nval, feats), f32),
            pltpu.VMEM((drows, nval + LANES), f32),
            pltpu.VMEM((N, drows, nval + LANES), f32),
            dma((2, 2)),
            dma((I - 1, nb)), dma((I - 1, nb)),
            dma((nb,)), dma((nb,)), dma((nb,)), dma((nb,)),
            dma((Q - 1,)), dma((Q - 1,)), dma,
            dma((N - 1,)), dma((N - 1,)), dma((N - 1,)), dma((N - 1,)),
        ],
        compiler_params=pltpu.CompilerParams(
            collective_id=0, has_side_effects=True, vmem_limit_bytes=60 * 1024 * 1024
        ),
    )(
        hidden_acts.reshape(p_here * seq, units_here),
        out_grads.reshape(p_here * seq, out_grads.shape[2]),
        proj_in.T, proj_out.T, lengths, val_grads,
    )


def solution(mesh):
    inner = 2 ** (int(math.log2(mesh.shape["units"])) // 2)
    in_specs = (
        P("prompts", None, "units"),
        P("prompts", None, "units"),
        P("units", None),
        P("units", None),
        P("prompts"),
        P("prompts", "units"),
    )
    return jax.shard_map(
        functools.partial(per_device, inner), mesh=mesh, in_specs=in_specs,
        out_specs=P("prompts", None), check_vma=False,
    )
```

```python
import functools
import math

import jax
import jax.numpy as jnp
from jax import lax
from jax.experimental import pallas as pl
from jax.experimental.pallas import tpu as pltpu
from jax.sharding import PartitionSpec as P

MESH = pl.DeviceIdType.MESH
HIGHEST = lax.Precision.HIGHEST
LANES = 128
SKEW = 3
EARLY = 3
OWNAT = 2
FIN = 0
SUB = 128


def kernel(
    cfg,
    acts, grads, win, wout, lens, val,
    out,
    abuf, gbuf, wi, wo, sx, own, rx, pre, suf, psend, ssend, macc, gsend, grecv, vall, dsend, drecv,
    t2, t2pre, t2suf, t2ps, t2ss, tt, rt, hbm_sem, x_s, x_r, pre_s, pre_r, suf_s, suf_r, v_s, v_r, v_l, g_s, g_r, d_s, d_r,
    p2_s, p2_r, s2_s, s2_r, x2_s, x2_r,
):
    N, I, O, Q = cfg["N"], cfg["I"], cfg["O"], cfg["Q"]
    ct, ncb, nb, spc = cfg["ct"], cfg["ncb"], cfg["nb"], cfg["spc"]
    seq, p_here, rank = cfg["seq"], cfg["p_here"], cfg["rank"]
    nc2, nb2 = cfg["nc2"], cfg["nb2"]
    per = nb2 // O
    rows_own = ncb * ct
    half = ct // 2
    K = I * ncb + nc2
    OWN2 = min(nb2 + OWNAT, nb - 1)
    me = lax.axis_index("units")
    q = lax.axis_index("prompts")
    o = me // I
    i = me % I

    barrier = pltpu.get_barrier_semaphore()
    for d in range(1, N):
        pl.semaphore_signal(barrier, inc=1, device_id={"units": (me + d) % N}, device_id_type=MESH)
    for d in range(1, Q):
        pl.semaphore_signal(barrier, inc=1, device_id={"prompts": (q + d) % Q}, device_id_type=MESH)

    def fetch(k):
        if isinstance(k, int) and 1 <= k <= nc2:
            row0 = I * rows_own + (k - 1) * ct
        else:
            kk = 0 if isinstance(k, int) and k == 0 else k - nc2
            owner = (i + 1 + kk // ncb) % I
            row0 = pl.multiple_of(owner * rows_own + (kk % ncb) * ct, ct)
        slot = k % 2
        return (
            pltpu.make_async_copy(acts.at[pl.ds(row0, ct)], abuf.at[slot], hbm_sem.at[slot, 0]),
            pltpu.make_async_copy(grads.at[pl.ds(row0, ct)], gbuf.at[slot], hbm_sem.at[slot, 1]),
        )

    for copy in fetch(0):
        copy.start()

    for w, dst in ((win, wi), (wout, wo)):
        t = w[...].astype(jnp.float32)
        zero = jnp.zeros_like(t)
        dst[0] = jnp.concatenate([t, zero], axis=0).T.astype(dst.dtype)
        dst[1] = jnp.concatenate([zero, t], axis=0).T.astype(dst.dtype)
    macc[...] = jnp.zeros_like(macc)

    vrows = val.shape[0]
    mine = vall.at[pl.ds(pl.multiple_of(q * vrows, vrows), vrows)]
    val_own = pltpu.make_async_copy(val, mine, v_l)
    val_own.start()

    def val_copy(d):
        return pltpu.make_async_remote_copy(
            src_ref=val, dst_ref=mine, send_sem=v_s.at[d - 1], recv_sem=v_r.at[d - 1],
            device_id={"prompts": (q + d) % Q}, device_id_type=MESH,
        )

    def project(k, store):
        if isinstance(k, int):
            for copy in fetch(k + 1):
                copy.start()
        else:
            @pl.when(k + 1 < K)
            def _():
                for copy in fetch(k + 1):
                    copy.start()

        for copy in fetch(k):
            copy.wait()
        slot = k % 2
        for side, (buf, w) in enumerate(((abuf, wi), (gbuf, wo))):
            part = jnp.dot(buf[slot, :half], w[0], preferred_element_type=jnp.float32)
            part += jnp.dot(buf[slot, half:], w[1], preferred_element_type=jnp.float32)
            for s in range(spc):
                store(s, side, part[s * SUB : (s + 1) * SUB])

    def x_copy(e, b):
        return pltpu.make_async_remote_copy(
            src_ref=sx.at[e, b], dst_ref=rx.at[e, b], send_sem=x_s.at[e, b], recv_sem=x_r.at[e, b],
            device_id={"units": o * I + (i + 1 + e) % I}, device_id_type=MESH,
        )

    def first_compute(k, kk):
        def store(s, side, x):
            sx[kk // ncb, (kk % ncb) * spc + s, side] = x

        project(k, store)

    def first_send(k):
        for s in range(spc):
            x_copy(k // ncb, (k % ncb) * spc + s).start()

    def first(kk, carry):
        first_compute(kk + nc2, kk)
        first_send(kk)
        return carry

    first_compute(0, 0)
    pl.semaphore_wait(barrier, N - 1 + Q - 1)
    first_send(0)
    for d in range(1, Q):
        val_copy(d).start()

    def right2(b, src):
        return pltpu.make_async_remote_copy(
            src_ref=src.at[b], dst_ref=t2pre.at[b], send_sem=p2_s.at[b], recv_sem=p2_r.at[b],
            device_id={"units": (me + I) % N}, device_id_type=MESH,
        )

    def left2(b, src):
        return pltpu.make_async_remote_copy(
            src_ref=src.at[b], dst_ref=t2suf.at[b], send_sem=s2_s.at[b], recv_sem=s2_r.at[b],
            device_id={"units": (me + N - I) % N}, device_id_type=MESH,
        )

    def x2_copy(e, n):
        to = (i + 1 + e) % I
        return pltpu.make_async_remote_copy(
            src_ref=tt.at[to * (per // I) + n], dst_ref=rt.at[e, n],
            send_sem=x2_s.at[e, n], recv_sem=x2_r.at[e, n],
            device_id={"units": o * I + to}, device_id_type=MESH,
        )

    for c2 in range(nc2):
        def store2(s, side, x, c2=c2):
            t2[c2 * spc + s, side] = x

        project(1 + c2, store2)

    if nc2:
        @pl.when(o == 0)
        def _():
            for b in range(nb2 - 1, max(per, nb2 - EARLY) - 1, -1):
                right2(b, t2).start()

        @pl.when(o == O - 1)
        def _():
            for b in range(min(nb2 - per, EARLY)):
                left2(b, t2).start()

    lax.fori_loop(1, (I - 1) * ncb, first, 0)

    def second(c, carry):
        def store(s, side, x):
            own[c * spc + s, side] = x

        project(nc2 + (I - 1) * ncb + c, store)
        return carry

    lax.fori_loop(0, ncb, second, 0)

    def relay2(t):
        ir = t - SKEW * o
        b = nb2 - 1 - ir
        il = t - SKEW * (O - 1 - o)

        @pl.when((o == 0) & (ir >= EARLY) & (ir < nb2 - per))
        def _():
            right2(b, t2).start()

        @pl.when((o > 0) & (ir >= 0) & (ir < nb2 - per * (o + 1)))
        def _():
            right2(b, t2ps).wait_recv()
            t2ps[b] = t2[b] + t2pre[b]
            right2(b, t2ps).start()

        @pl.when((o == O - 1) & (il >= EARLY) & (il < nb2 - per))
        def _():
            left2(il, t2).start()

        @pl.when((o < O - 1) & (il >= 0) & (il < per * o))
        def _():
            left2(il, t2ss).wait_recv()
            t2ss[il] = t2[il] + t2suf[il]
            left2(il, t2ss).start()

    def own2():
        for m in range(per):
            b = o * per + m
            tt[m] = t2[b]

            @pl.when(o > 0)
            def _():
                right2(b, t2ps).wait_recv()
                tt[m] += t2pre[b]

            @pl.when(o < O - 1)
            def _():
                left2(b, t2ss).wait_recv()
                tt[m] += t2suf[b]

        for e in range(I - 1):
            for n in range(per // I):
                x2_copy(e, n).start()

    def masked(g, p, pos0):
        pos = pos0 + lax.broadcasted_iota(jnp.int32, (SUB, LANES), 0)
        lane = lax.broadcasted_iota(jnp.int32, (SUB, LANES), 1)
        return jnp.where(pos + jnp.where(lane < rank, 0, half) < lens[p], g, 0.0)

    def gram(a, g):
        return lax.dot_general(
            a, g, (((0,), (0,)), ((), ())), precision=HIGHEST, preferred_element_type=jnp.float32
        )

    def right_copy(b):
        return pltpu.make_async_remote_copy(
            src_ref=psend.at[b], dst_ref=pre.at[b], send_sem=pre_s.at[b], recv_sem=pre_r.at[b],
            device_id={"units": (me + I) % N}, device_id_type=MESH,
        )

    def left_copy(b):
        return pltpu.make_async_remote_copy(
            src_ref=ssend.at[b], dst_ref=suf.at[b], send_sem=suf_s.at[b], recv_sem=suf_r.at[b],
            device_id={"units": (me + N - I) % N}, device_id_type=MESH,
        )

    def third(t, carry):
        @pl.when(t < nb)
        def _():
            for e in range(I - 1):
                x_copy(e, t).wait_recv()
            a = own[t, 0]
            g = own[t, 1]
            for e in range(I - 1):
                a += rx[e, t, 0]
                g += rx[e, t, 1]
            own[t, 0] = a
            tok0 = i * rows_own + (t // spc) * ct
            own[t, 1] = masked(g, tok0 // seq, tok0 % seq + (t % spc) * SUB)

        br = t - SKEW * o

        @pl.when((br >= 0) & (br < nb))
        def _():
            @pl.when(o == 0)
            def _():
                psend[br] = own[br, 0]

            @pl.when(o > 0)
            def _():
                right_copy(br).wait_recv()
                psend[br] = own[br, 0] + pre[br]

            @pl.when(o < O - 1)
            def _():
                right_copy(br).start()

        bl = t - SKEW * (O - 1 - o)

        @pl.when((bl >= 0) & (bl < nb))
        def _():
            @pl.when(o == O - 1)
            def _():
                ssend[bl] = own[bl, 0]

            @pl.when(o < O - 1)
            def _():
                left_copy(bl).wait_recv()
                ssend[bl] = own[bl, 0] + suf[bl]

            @pl.when(o > 0)
            def _():
                left_copy(bl).start()

        if nc2:
            @pl.when(t < nb)
            def _():
                relay2(t)

            @pl.when(t == OWN2)
            def _():
                own2()

        b = t - SKEW * (O - 1)

        @pl.when(b >= 0)
        def _():
            def add(x):
                p = (i * rows_own + (b // spc) * ct) // seq
                macc[p] += gram(x, own[b, 1])

            @pl.when(o < O - 1)
            def _():
                add(psend[b] + suf[b])

            @pl.when(o == O - 1)
            def _():
                add(psend[b])

        if nc2:
            @pl.when(t == nb + FIN)
            def _():
                for n in range(per // I):
                    mine2 = i * (per // I) + n
                    x = tt[mine2]
                    for e in range(I - 1):
                        x2_copy(e, n).wait_recv()
                        x += rt[e, n]
                    blk = o * per + mine2
                    p = p_here - 1
                    macc[p] += gram(x[0], masked(x[1], p, (blk // spc) * ct + (blk % spc) * SUB))

        return carry

    lax.fori_loop(0, nb + SKEW * (O - 1), third, 0)

    grows = gsend.shape[2]
    for p in range(p_here):
        m = macc[p]
        g = m[:rank, :rank] + m[rank:, rank:]
        g2 = jnp.concatenate([g, g], axis=1)
        for n in range(N):
            gsend[n, p] = g2[n * grows : (n + 1) * grows]

    def g_copy(d):
        to = (me + d) % N
        return pltpu.make_async_remote_copy(
            src_ref=gsend.at[to], dst_ref=grecv.at[me], send_sem=g_s.at[d - 1], recv_sem=g_r.at[d - 1],
            device_id={"units": to}, device_id_type=MESH,
        )

    for d in range(1, N):
        g_copy(d).start()
    grecv[me] = gsend[me]
    val_own.wait()
    for d in range(1, Q):
        val_copy(d).wait()
    for d in range(1, N):
        g_copy(d).wait()

    lane = lax.broadcasted_iota(jnp.int32, (1, LANES), 1)
    rows = []
    for p in range(p_here):
        s = grecv[0, p]
        for n in range(1, N):
            s += grecv[n, p]
        flat = [
            jnp.where(lane < rank, s[2 * r : 2 * r + 1], s[2 * r + 1 : 2 * r + 2])
            for r in range(grows // 2)
        ]
        rows.append(jnp.concatenate(flat, axis=1))
    pad = dsend.shape[0] - p_here
    feat = jnp.concatenate(rows + [jnp.zeros((pad, rows[0].shape[1]), jnp.float32)], axis=0)
    nval = vall.shape[0]
    dsend[:, :nval] = lax.dot_general(
        feat, vall[...], (((1,), (1,)), ((), ())), precision=HIGHEST,
        preferred_element_type=jnp.float32,
    )
    dsend[:, nval:] = jnp.broadcast_to(
        jnp.sum(feat * feat, axis=1, keepdims=True), (dsend.shape[0], LANES)
    )

    def d_copy(d):
        return pltpu.make_async_remote_copy(
            src_ref=dsend, dst_ref=drecv.at[me], send_sem=d_s.at[d - 1], recv_sem=d_r.at[d - 1],
            device_id={"units": (me + d) % N}, device_id_type=MESH,
        )

    for d in range(1, N):
        d_copy(d).start()
    drecv[me] = dsend[...]

    def drain(b, carry):
        for e in range(I - 1):
            x_copy(e, b).wait_send()

        @pl.when(o < O - 1)
        def _():
            right_copy(b).wait_send()

        @pl.when(o > 0)
        def _():
            left_copy(b).wait_send()

        return carry

    lax.fori_loop(0, nb, drain, 0)

    def drain2(b, carry):
        @pl.when(o < b // per)
        def _():
            right2(b, t2ps).wait_send()

        @pl.when(o > b // per)
        def _():
            left2(b, t2ss).wait_send()

        return carry

    if nc2:
        lax.fori_loop(0, nb2, drain2, 0)
        for e in range(I - 1):
            for n in range(per // I):
                x2_copy(e, n).wait_send()
    for d in range(1, N):
        d_copy(d).wait()
    total = drecv[0]
    for n in range(1, N):
        total += drecv[n]
    out[...] = total[:p_here, :nval] / jnp.sqrt(total[:p_here, nval : nval + 1] + 1e-06)


def per_device(inner, hidden_acts, out_grads, proj_in, proj_out, lengths, val_grads):
    p_here, seq, units_here = hidden_acts.shape
    rank = proj_in.shape[1]
    N, Q = lax.axis_size("units"), lax.axis_size("prompts")
    I = inner
    O = N // I
    ct = min(1024, seq)
    nb2 = seq // 2 // SUB
    nc2 = seq // ct
    if p_here < 2 or (p_here - 1) * seq % (I * ct) or nb2 % (O * I):
        nc2 = nb2 = 0
    rows_own = (p_here * seq - nc2 * ct) // I
    ncb = rows_own // ct
    spc = ct // 2 // SUB
    nb = ncb * spc
    feats = val_grads.shape[1]
    grows = feats // rank
    nval = val_grads.shape[0] * Q
    cfg = dict(
        N=N, I=I, O=O, Q=Q, ct=ct, ncb=ncb, nb=nb, spc=spc, seq=seq, p_here=p_here, rank=rank, nc2=nc2,
        nb2=nb2,
    )
    f32 = jnp.float32
    dma = pltpu.SemaphoreType.DMA
    block = (SUB, LANES)
    drows = -(-p_here // 8) * 8
    vmem = pl.BlockSpec(memory_space=pltpu.VMEM)
    hbm = pl.BlockSpec(memory_space=pl.ANY)
    return pl.pallas_call(
        functools.partial(kernel, cfg),
        out_shape=jax.ShapeDtypeStruct((p_here, nval), f32),
        in_specs=[hbm, hbm, vmem, vmem, pl.BlockSpec(memory_space=pltpu.SMEM), vmem],
        out_specs=vmem,
        scratch_shapes=[
            pltpu.VMEM((2, ct, units_here), hidden_acts.dtype),
            pltpu.VMEM((2, ct, out_grads.shape[2]), out_grads.dtype),
            pltpu.VMEM((2, units_here, LANES), proj_in.dtype),
            pltpu.VMEM((2, out_grads.shape[2], LANES), proj_out.dtype),
            pltpu.VMEM((I - 1, nb, 2) + block, f32),
            pltpu.VMEM((nb, 2) + block, f32),
            pltpu.VMEM((I - 1, nb, 2) + block, f32),
            pltpu.VMEM((nb,) + block, f32),
            pltpu.VMEM((nb,) + block, f32),
            pltpu.VMEM((nb,) + block, f32),
            pltpu.VMEM((nb,) + block, f32),
            pltpu.VMEM((p_here, LANES, LANES), f32),
            pltpu.VMEM((N, p_here, grows, LANES), f32),
            pltpu.VMEM((N, p_here, grows, LANES), f32),
            pltpu.VMEM((nval, feats), f32),
            pltpu.VMEM((drows, nval + LANES), f32),
            pltpu.VMEM((N, drows, nval + LANES), f32),
            *[pltpu.VMEM((max(nb2, 1), 2) + block, f32)] * 5,
            pltpu.VMEM((max(nb2 // O, 1), 2) + block, f32),
            pltpu.VMEM((I - 1, max(nb2 // N, 1), 2) + block, f32),
            dma((2, 2)),
            dma((I - 1, nb)), dma((I - 1, nb)),
            dma((nb,)), dma((nb,)), dma((nb,)), dma((nb,)),
            dma((Q - 1,)), dma((Q - 1,)), dma,
            dma((N - 1,)), dma((N - 1,)), dma((N - 1,)), dma((N - 1,)),
            *[dma((max(nb2, 1),))] * 4,
            *[dma((I - 1, max(nb2 // N, 1)))] * 2,
        ],
        compiler_params=pltpu.CompilerParams(
            collective_id=0, has_side_effects=True, vmem_limit_bytes=60 * 1024 * 1024
        ),
    )(
        hidden_acts.reshape(p_here * seq, units_here),
        out_grads.reshape(p_here * seq, out_grads.shape[2]),
        proj_in.T, proj_out.T, lengths, val_grads,
    )


def solution(mesh):
    inner = 2 ** (int(math.log2(mesh.shape["units"])) // 2)
    in_specs = (
        P("prompts", None, "units"),
        P("prompts", None, "units"),
        P("units", None),
        P("units", None),
        P("prompts"),
        P("prompts", "units"),
    )
    return jax.shard_map(
        functools.partial(per_device, inner), mesh=mesh, in_specs=in_specs,
        out_specs=P("prompts", None), check_vma=False,
    )
```
